32 devices in a mesh: groups: 2 (over y), mem: 4 (over x, core), heads: 4 (over z).
Axes of the slice: x: 2, y: 2, z: 4, core: 2. Of those that a mesh axis runs over, the one named last changes fastest.
Arguments:
- hidden: bfloat16 [32, 8192], P(('groups', 'heads')), parts along dimension 0, may hold values from -6 to 6
- norm_gain: bfloat16 [8192], P('mem'), may hold values from 0.5 to 1.5
- q_weight: bfloat16 [8192, 8192], P('mem', 'heads'), may hold values from -0.0625 to 0.0625
- k_weight: bfloat16 [8192, 1024], P('mem', 'heads'), may hold values from -1 to 1, as said below
- v_weight: bfloat16 [8192, 1024], P('mem', 'heads'), may hold values from -1 to 1, as said below
- o_weight: bfloat16 [8192, 8192], P('heads', 'mem'), may hold values from -0.0625 to 0.0625
- k_cache: bfloat16 [384, 8, 128, 128], P(('groups', 'mem'), 'heads'), parts along dimension 0, may hold values from -40 to 40, as said below
- v_cache: bfloat16 [384, 8, 128, 128], P(('groups', 'mem'), 'heads'), parts along dimension 0, may hold values from -6 to 6, as said below
- page_table: int32 [16, 24], P('groups'), parts along dimension 0, may hold values from 0 to 191, as said below
- attend_list: int32 [16, 8], P('groups'), parts along dimension 0, may hold values from 0 to 23, as said below
- lengths: int32 [16], P('groups'), parts along dimension 0, may hold values from 1409 to 3072, as said below
Outputs:
- layer_out: bfloat16 [32, 8192], P(('groups', 'heads'), 'mem'), parts along dimension 0
The draws below stay inside these ranges and needn't reach their ends.
There are 2 independent parts, one for each index of `groups`. The reference program is written for one: setup_inputs(seed, part) draws one part's arguments, and reference() takes and returns one part's arrays. A program takes and returns all parts, laid end to end along the dimension named above; an argument that names none is the same for every part. Nothing has to cross between parts.
Inputs may be any that keep to these rules, and one draw needn't show every extreme that they name: `page_table`: A permutation of the pool slots 0 to 191 laid out as 8 rows of 24. The blocks named by attend_list lie at most 32 in any one range of slots m * 48 to (m + 1) * 48 - 1, and exactly 32 in some such range. `attend_list`: each row names 8 distinct blocks, all below ceil(lengths[r] / 128), among them its last block ceil(lengths[r] / 128) - 1. `lengths`: some row holds 3072 steps. `k_cache`: each key-value head is stored 1 times, the copies equal. `v_cache`: each key-value head is stored 1 times, the copies equal. `k_weight`: the 1 column blocks of each key-value head are equal. `v_weight`: the 1 column blocks of each key-value head are equal.
All inputs are finite; a program needn't handle non-finite values.
Results may differ from the reference program's by a relative error of at most 0.007.
The reference program's roundings to bfloat16 on the way count: a program that leaves them out, or rounds other values in their place, can miss the bound.
Values may be sent and summed in bfloat16 or wider, within the bound.
A program may use at most 64 MiB of HBM per device.

```python
import jax
import jax.numpy as jnp
from jax import lax

D = 8192
HQ = 64
KVH = 8
HD = 128
BS = 128
STEPS = 2
ROWS = 8
BLK_DEV = 48
NBLK = 192
HBLK = 24
SEL = 8
CAP = 32
KVC = 8
REP = 1
TOKENS = 16


def layout_tables(key):
    base_key = jax.random.fold_in(key, 7)
    key_blocks, key_longest, key_tail, key_pick, key_rank, key_slots, key_pairs = jax.random.split(base_key, 7)
    row_ids = jnp.arange(ROWS, dtype=jnp.int32)
    lowest = max(SEL, HBLK // 2)
    block_count = jax.random.randint(key_blocks, (ROWS,), lowest, HBLK + 1).astype(jnp.int32)
    longest = jax.random.randint(key_longest, (), 0, ROWS)
    block_count = jnp.where(row_ids == longest, HBLK, block_count)
    tail_steps = jax.random.randint(key_tail, (ROWS,), 1, BS + 1).astype(jnp.int32)
    tail_steps = jnp.where(row_ids == longest, BS, tail_steps)
    row_lengths = (block_count - 1) * BS + tail_steps
    block_ids = jnp.arange(HBLK, dtype=jnp.int32)
    pick_score = jax.random.randint(key_pick, (ROWS, HBLK), 0, 1 << 20).astype(jnp.int32) * HBLK + block_ids[None, :]
    pick_score = jnp.where(block_ids[None, :] < block_count[:, None] - 1, pick_score, (1 << 20) * HBLK + HBLK + block_ids[None, :])
    pick_score = jnp.where(block_ids[None, :] == block_count[:, None] - 1, -1, pick_score)
    chosen_blocks = jnp.argsort(pick_score, axis=1)[:, :SEL].astype(jnp.int32)
    attended = jnp.any(chosen_blocks[:, :, None] == block_ids[None, None, :], axis=1).reshape(-1)
    owners = NBLK // BLK_DEV
    listed = ROWS * SEL
    spread = (listed - CAP) // (owners - 1)
    extra = listed - CAP - spread * (owners - 1)
    owner_rank = jax.random.permutation(key_rank, owners).astype(jnp.int32)
    owner_load = jnp.where(owner_rank == 0, CAP, spread + (owner_rank <= extra).astype(jnp.int32))
    slot_ids = jnp.arange(BLK_DEV, dtype=jnp.int32)
    inner_order = jnp.argsort(jax.random.randint(key_slots, (owners, BLK_DEV), 0, 1 << 20).astype(jnp.int32) * BLK_DEV + slot_ids[None, :], axis=1).astype(jnp.int32)
    owner_ids = jnp.arange(owners, dtype=jnp.int32)[:, None]
    slot_values = (owner_ids * BLK_DEV + inner_order).reshape(-1)
    slot_used = (slot_ids[None, :] < owner_load[:, None]).reshape(-1)
    slot_order = jnp.argsort(jnp.where(slot_used, 0, NBLK) + jnp.arange(NBLK, dtype=jnp.int32))
    pair_rank = jax.random.permutation(key_pairs, NBLK).astype(jnp.int32)
    pair_order = jnp.argsort(jnp.where(attended, 0, NBLK) + pair_rank)
    table = jnp.zeros((NBLK,), jnp.int32).at[pair_order].set(slot_values[slot_order])
    return (table.reshape(ROWS, HBLK), chosen_blocks, row_lengths.astype(jnp.int32))


def draw_page_table(key, part):
    return layout_tables(key)[0]


def draw_attend_list(key, part):
    return layout_tables(key)[1]


def draw_lengths(key, part):
    return layout_tables(key)[2]


def draw_k_cache(key, part):
    key_base = jax.random.fold_in(jax.random.fold_in(key, 11), 0)
    values = jnp.clip(jax.random.normal(key_base, (NBLK, KVH, BS, HD), jnp.float32), -6.0, 6.0)
    return jnp.repeat(values, REP, axis=1).astype(jnp.bfloat16)


def draw_v_cache(key, part):
    values = jnp.clip(jax.random.normal(jax.random.fold_in(key, 13), (NBLK, KVH, BS, HD), jnp.float32), -6.0, 6.0)
    return jnp.repeat(values, REP, axis=1).astype(jnp.bfloat16)


def duplicated_weight(key, salt, factor):
    values = jnp.clip(jax.random.normal(jax.random.fold_in(key, salt), (D, KVH, 1, HD), jnp.float32), -4.0, 4.0) * (factor * D ** (-0.5))
    return jnp.broadcast_to(values, (D, KVH, REP, HD)).reshape(D, KVC * HD).astype(jnp.bfloat16)


def draw_k_weight(key, part):
    return duplicated_weight(key, 17, 4.0)


def draw_v_weight(key, part):
    return duplicated_weight(key, 19, 3.0)


def shard_levels(stream_key, shape, shards, least, top_value):
    factor_of = 1.0
    for dim, parts in shards:
        heights = jax.random.uniform(jax.random.fold_in(jax.random.fold_in(stream_key, 6), dim), (parts,), jnp.float32, least / len(shards), top_value / len(shards))
        factor_of = factor_of * jnp.repeat(jnp.exp(heights), shape[dim] // parts).reshape((-1,) + (1,) * (len(shape) - 1 - dim))
    return factor_of


def bell_draw(stream_key, dims, width, limit, cuts=(), held_as=jnp.bfloat16):
    drawn = width * jax.random.normal(stream_key, dims, jnp.float32)
    if cuts:
        drawn = drawn * shard_levels(stream_key, dims, cuts, -0.22, 0.18)
    return jnp.clip(drawn, -limit, limit).astype(held_as)


def setup_inputs(seed: int = 0, part: int = 0) -> dict:
    key_of = jax.random.split(jax.random.key(seed), 12)
    part_keys = jax.random.split(jax.random.fold_in(key_of[11], part), 12)
    hidden = bell_draw(part_keys[0], (TOKENS, D), 1.0, 6.0, ((0, 4),))
    norm_gain = jnp.clip(1.0 + 0.1 * jax.random.normal(key_of[1], (D,), jnp.float32), 0.5, 1.5).astype(jnp.bfloat16)
    q_weight = bell_draw(key_of[2], (D, HQ * HD), D ** -0.5, 0.0625, ((0, 4), (1, 4)))
    k_weight = draw_k_weight(jax.random.fold_in(key_of[11], 71), part)
    v_weight = draw_v_weight(jax.random.fold_in(key_of[11], 71), part)
    o_weight = bell_draw(key_of[5], (HQ * HD, D), (HQ * HD) ** -0.5, 0.0625, ((0, 4), (1, 4)))
    k_cache = draw_k_cache(jax.random.fold_in(jax.random.fold_in(key_of[11], part), 71), part)
    v_cache = draw_v_cache(jax.random.fold_in(jax.random.fold_in(key_of[11], part), 71), part)
    page_table = draw_page_table(jax.random.fold_in(jax.random.fold_in(key_of[11], part), 71), part)
    attend_list = draw_attend_list(jax.random.fold_in(jax.random.fold_in(key_of[11], part), 71), part)
    lengths = draw_lengths(jax.random.fold_in(jax.random.fold_in(key_of[11], part), 71), part)
    return dict(hidden=hidden, norm_gain=norm_gain, q_weight=q_weight, k_weight=k_weight, v_weight=v_weight, o_weight=o_weight, k_cache=k_cache, v_cache=v_cache, page_table=page_table, attend_list=attend_list, lengths=lengths)


def reference(hidden, norm_gain, q_weight, k_weight, v_weight, o_weight, k_cache, v_cache, page_table, attend_list, lengths):
    hidden_f = hidden.astype(jnp.float32)
    mean_sq = lax.optimization_barrier(jnp.mean(hidden_f * hidden_f, axis=-1, keepdims=True))
    normed = (hidden_f * lax.rsqrt(mean_sq + 1e-05) * norm_gain.astype(jnp.float32)).astype(jnp.bfloat16)
    group_size = HQ // KVH
    queries = jnp.dot(normed, q_weight, preferred_element_type=jnp.float32).astype(jnp.bfloat16)
    queries = queries.reshape(ROWS, STEPS, KVH, group_size, HD)
    key_base = k_weight.reshape(D, KVH, REP, HD)[:, :, 0, :].reshape(D, KVH * HD)
    value_base = v_weight.reshape(D, KVH, REP, HD)[:, :, 0, :].reshape(D, KVH * HD)
    new_keys = jnp.dot(normed, key_base, preferred_element_type=jnp.float32).astype(jnp.bfloat16).reshape(ROWS, STEPS, KVH, HD)
    new_values = jnp.dot(normed, value_base, preferred_element_type=jnp.float32).astype(jnp.bfloat16).reshape(ROWS, STEPS, KVH, HD)
    cache_keys = k_cache[:, ::REP]
    cache_values = v_cache[:, ::REP]
    scale_factor = HD ** (-0.5)
    highest = lax.Precision.HIGHEST

    def one_row(operands):
        row_query, row_keys, row_values, table_row, list_row, row_length = operands
        slots = jnp.take(table_row, list_row).astype(jnp.int32)
        block_keys = jnp.take(cache_keys, slots, axis=0).astype(jnp.float32)
        block_values = jnp.take(cache_values, slots, axis=0).astype(jnp.float32)
        positions = list_row[:, None] * BS + jnp.arange(BS, dtype=jnp.int32)[None, :]
        valid = positions < row_length
        query_f = row_query.astype(jnp.float32)
        cache_scores = jnp.einsum('sgpd,ngkd->sgpnk', query_f, block_keys, precision=highest) * scale_factor
        cache_scores = jnp.where(valid[None, None, None], cache_scores, -jnp.inf)
        cache_scores = cache_scores.reshape(STEPS, KVH, group_size, SEL * BS)
        fresh_scores = jnp.einsum('sgpd,tgd->sgpt', query_f, row_keys.astype(jnp.float32), precision=highest) * scale_factor
        causal = jnp.arange(STEPS, dtype=jnp.int32)[None, :] <= jnp.arange(STEPS, dtype=jnp.int32)[:, None]
        fresh_scores = jnp.where(causal[:, None, None, :], fresh_scores, -jnp.inf)
        all_scores = jnp.concatenate([cache_scores, fresh_scores], axis=-1)
        row_peak = lax.optimization_barrier(jnp.max(all_scores, axis=-1, keepdims=True))
        weights = jnp.exp(all_scores - row_peak)
        weight_sum = lax.optimization_barrier(jnp.sum(weights, axis=-1, keepdims=True))
        all_values = jnp.concatenate([block_values.transpose(1, 0, 2, 3).reshape(KVH, SEL * BS, HD), row_values.astype(jnp.float32).transpose(1, 0, 2)], axis=1)
        mixed = jnp.einsum('sgpk,gkd->sgpd', weights, all_values, precision=highest)
        return (mixed / weight_sum).astype(jnp.bfloat16).reshape(STEPS, HQ * HD)
    attended = lax.map(one_row, (queries, new_keys, new_values, page_table, attend_list, lengths))
    attended = attended.reshape(ROWS * STEPS, HQ * HD)
    return jnp.dot(attended, o_weight, preferred_element_type=jnp.float32).astype(jnp.bfloat16)
```

```python
import functools

import jax
import jax.numpy as jnp
from jax import lax
from jax.experimental import pallas as pl
from jax.experimental.pallas import tpu as pltpu
from jax.sharding import PartitionSpec as P

MESH = pl.DeviceIdType.MESH
NEG_FILL = -1e30
EPSILON = 1e-05
PIECES = 4
F32 = jnp.float32
BF16 = jnp.bfloat16


def layer_kernel(
    mem_count,
    head_count,
    chunks,
    page_ref,
    attend_ref,
    length_ref,
    hidden_ref,
    gain_ref,
    wq_hbm,
    wk_hbm,
    wv_hbm,
    wo_hbm,
    kc_hbm,
    vc_hbm,
    out_ref,
    wq,
    wk,
    wv,
    wo,
    kc,
    vc,
    norm_buf,
    part,
    part_in,
    own_heads,
    heads_all,
    row_queries,
    accum,
    accum_in,
    stat_in,
    own_att,
    att_all,
    proj,
    proj_in,
    load_sem,
    norm_send,
    norm_recv,
    part_send,
    part_recv,
    heads_send,
    heads_recv,
    accum_send,
    accum_recv,
    stat_send,
    stat_recv,
    att_send,
    att_recv,
    proj_send,
    proj_recv,
):
    mem = lax.axis_index("mem")
    head = lax.axis_index("heads")
    row_count, sel = attend_ref.shape
    features = wq.shape[0]
    q_cols, kv_cols = wq.shape[1], wk.shape[1]
    pool, local_kv, block, dim = kc.shape
    tokens = accum.shape[0]
    steps = tokens // row_count
    own_tokens = tokens // mem_count
    head_tokens = tokens // head_count
    local_heads = q_cols // dim
    per_kv = local_heads // local_kv
    queries = steps * per_kv
    scale = dim ** (-0.5)

    def mem_peer(k):
        return lax.rem(mem + k, mem_count)

    def mem_source(k):
        return lax.rem(mem + mem_count - k, mem_count)

    def head_peer(k):
        return lax.rem(head + k, head_count)

    def head_source(k):
        return lax.rem(head + head_count - k, head_count)

    loads = []
    for which, (source, target) in enumerate(
        ((wk_hbm, wk), (wv_hbm, wv), (wq_hbm, wq), (kc_hbm, kc), (vc_hbm, vc), (wo_hbm, wo))
    ):
        rows = source.shape[0] // PIECES
        group = []
        for piece in range(PIECES):
            view = pl.ds(piece * rows, rows)
            copy = pltpu.make_async_copy(
                source.at[view], target.at[view], load_sem.at[which, piece]
            )
            copy.start()
            group.append(copy)
        loads.append(group)

    def arrive(which):
        for copy in loads[which]:
            copy.wait()

    barrier = pltpu.get_barrier_semaphore()
    for k in range(1, mem_count):
        pl.semaphore_signal(barrier, inc=1, device_id={"mem": mem_peer(k)}, device_id_type=MESH)
    for k in range(1, head_count):
        pl.semaphore_signal(barrier, inc=1, device_id={"heads": head_peer(k)}, device_id_type=MESH)

    hidden = hidden_ref[...].astype(F32)
    mean_sq = jnp.mean(hidden * hidden, axis=-1, keepdims=True)
    own = hidden_ref[:, pl.ds(pl.multiple_of(mem * features, 128), features)].astype(F32)
    normed = own * lax.rsqrt(mean_sq + EPSILON) * gain_ref[...].astype(F32)
    norm_buf[head] = normed.astype(BF16)

    pl.semaphore_wait(barrier, mem_count + head_count - 2)

    def norm_copy(k, slot):
        return pltpu.make_async_remote_copy(
            norm_buf.at[slot],
            norm_buf.at[slot],
            norm_send.at[k],
            norm_recv.at[k],
            device_id={"heads": head_peer(k)},
            device_id_type=MESH,
        )

    for k in range(head_count - 1, 0, -1):
        norm_copy(k, head).start()
    for k in range(1, head_count):
        norm_copy(k, head_source(k)).wait_recv()
    lhs = jnp.concatenate([norm_buf[i].astype(F32) for i in range(head_count)], axis=0).astype(BF16)

    def part_copy(index, start, width, k, target, slot):
        view = pl.ds(start, width)
        return pltpu.make_async_remote_copy(
            part.at[target, :, view],
            part_in.at[slot, :, view],
            part_send.at[index, k],
            part_recv.at[index, k],
            device_id={"mem": mem_peer(k)},
            device_id_type=MESH,
        )

    chunk = q_cols // chunks
    pieces = [(index, index * chunk, chunk) for index in range(chunks)]
    pieces.append((chunks, q_cols, 2 * kv_cols))

    arrive(0)
    arrive(1)
    fresh = jnp.concatenate(
        [
            jnp.dot(lhs, wk[...], preferred_element_type=F32),
            jnp.dot(lhs, wv[...], preferred_element_type=F32),
        ],
        axis=1,
    )
    for owner in range(mem_count):
        part[owner, :, q_cols:] = fresh[owner * own_tokens : (owner + 1) * own_tokens]
    for k in range(1, mem_count):
        part_copy(chunks, q_cols, 2 * kv_cols, k, mem_peer(k), mem).start()
    arrive(2)
    for index, start, width in pieces[:-1]:
        view = pl.ds(start, width)
        value = jnp.dot(lhs, wq[:, view], preferred_element_type=F32)
        for owner in range(mem_count):
            part[owner, :, view] = value[owner * own_tokens : (owner + 1) * own_tokens]
        for k in range(1, mem_count):
            part_copy(index, start, width, k, mem_peer(k), mem).start()

    total = part[mem]
    for k in range(1, mem_count):
        for index, start, width in pieces:
            part_copy(index, start, width, k, mem_peer(k), mem_source(k)).wait_recv()
        total = total + part_in[mem_source(k)]
    all_heads = local_heads + 2 * local_kv
    for h in range(all_heads):
        own_heads[:, h, :] = total[:, h * dim : (h + 1) * dim]
    heads_all[mem] = own_heads[...].astype(BF16)

    def heads_copy(k, slot):
        return pltpu.make_async_remote_copy(
            heads_all.at[slot],
            heads_all.at[slot],
            heads_send.at[k],
            heads_recv.at[k],
            device_id={"mem": mem_peer(k)},
            device_id_type=MESH,
        )

    for k in range(1, mem_count):
        heads_copy(k, mem).start()
    for k in range(1, mem_count):
        heads_copy(k, mem_source(k)).wait_recv()

    for r in range(row_count):
        token_heads = []
        for s in range(steps):
            t = r * steps + s
            token_heads.append(heads_all[t // own_tokens, t % own_tokens].astype(F32))
        for g in range(local_kv):
            row_queries[r, g] = jnp.concatenate(
                [value[g * per_kv : (g + 1) * per_kv] for value in token_heads], axis=0
            ).astype(BF16)

    arrive(3)
    arrive(4)
    lane = lax.broadcasted_iota(jnp.int32, (queries, dim), 1)
    key_lane = lax.broadcasted_iota(jnp.int32, (queries, block), 1)

    def attend_row(r, stat):
        slots, counts = [], []
        for j in range(sel):
            named = attend_ref[r, j]
            slot = page_ref[r, named] - mem * pool
            local = (slot >= 0) & (slot < pool)
            slots.append(jnp.clip(slot, 0, pool - 1))
            counts.append(jnp.where(local, length_ref[r] - named * block, 0))
        for g in range(local_kv):
            keys = jnp.concatenate([kc[slot, g] for slot in slots], axis=0)
            scores = lax.dot_general(
                row_queries[r, g],
                keys,
                (((1,), (1,)), ((), ())),
                preferred_element_type=F32,
            )
            valid = [key_lane < count for count in counts]
            kept = [
                jnp.where(valid[j], scores[:, j * block : (j + 1) * block] * scale, NEG_FILL)
                for j in range(sel)
            ]
            peak = jnp.max(functools.reduce(jnp.maximum, kept), axis=1, keepdims=True)
            weights = [jnp.where(valid[j], jnp.exp(kept[j] - peak), 0.0) for j in range(sel)]
            mass = jnp.sum(functools.reduce(jnp.add, weights), axis=1, keepdims=True)
            high = [w.astype(BF16) for w in weights]
            low = [(w - h.astype(F32)).astype(BF16) for w, h in zip(weights, high)]
            both = jnp.concatenate(
                [jnp.concatenate(high, axis=1), jnp.concatenate(low, axis=1)], axis=0
            )
            values = jnp.concatenate([vc[slot, g] for slot in slots], axis=0)
            mixed = jnp.dot(both, values, preferred_element_type=F32)
            mixed = mixed[:queries] + mixed[queries:]
            for s in range(steps):
                accum[r * steps + s, g] = mixed[s * per_kv : (s + 1) * per_kv]
            spot = r * local_kv + g
            stat = jnp.where(lane == spot, peak, stat)
            stat = jnp.where(lane == spot + row_count * local_kv, mass, stat)
        return stat

    stat = lax.fori_loop(0, row_count, attend_row, jnp.zeros((queries, dim), F32))
    for s in range(steps):
        stat_in[mem, s] = stat[s * per_kv : (s + 1) * per_kv]

    def stat_copy(k, slot):
        return pltpu.make_async_remote_copy(
            stat_in.at[slot],
            stat_in.at[slot],
            stat_send.at[k],
            stat_recv.at[k],
            device_id={"mem": mem_peer(k)},
            device_id_type=MESH,
        )

    def accum_copy(k, target, slot):
        return pltpu.make_async_remote_copy(
            accum.at[pl.ds(target * own_tokens, own_tokens)],
            accum_in.at[slot],
            accum_send.at[k],
            accum_recv.at[k],
            device_id={"mem": mem_peer(k)},
            device_id_type=MESH,
        )

    for k in range(1, mem_count):
        stat_copy(k, mem).start()
        accum_copy(k, mem_peer(k), mem).start()
    accum_in[mem] = accum[pl.ds(mem * own_tokens, own_tokens)]

    fresh_parts = []
    stat_lane = lax.broadcasted_iota(jnp.int32, (per_kv, dim), 1)
    for tl in range(own_tokens):
        t = mem * own_tokens + tl
        r, s = t // steps, t % steps
        own_query = heads_all[mem, tl].astype(F32)
        row_heads = []
        for u in range(steps):
            tu = r * steps + u
            row_heads.append(heads_all[tu // own_tokens, tu % own_tokens].astype(F32))
        for g in range(local_kv):
            query = own_query[g * per_kv : (g + 1) * per_kv]
            scores, new_values = [], []
            for u in range(steps):
                at = local_heads + g
                key = row_heads[u][at : at + 1]
                at = local_heads + local_kv + g
                new_values.append(row_heads[u][at : at + 1])
                score = jnp.sum(query * key, axis=1, keepdims=True) * scale
                seen = jnp.broadcast_to(s, (per_kv, 1)) >= u
                scores.append(jnp.where(seen, score, NEG_FILL))
            top = functools.reduce(jnp.maximum, scores)
            fresh_parts.append((r, s, scores, top, new_values))

    for k in range(1, mem_count):
        stat_copy(k, mem_source(k)).wait_recv()
        accum_copy(k, mem_peer(k), mem_source(k)).wait_recv()

    for tl in range(own_tokens):
        for g in range(local_kv):
            r, s, scores, top, new_values = fresh_parts[tl * local_kv + g]
            spot = r * local_kv + g
            stats = [stat_in[d, s] for d in range(mem_count)]
            peaks = [
                jnp.sum(jnp.where(stat_lane == spot, x, 0.0), axis=1, keepdims=True) for x in stats
            ]
            masses = [
                jnp.sum(
                    jnp.where(stat_lane == spot + row_count * local_kv, x, 0.0),
                    axis=1,
                    keepdims=True,
                )
                for x in stats
            ]
            peak = functools.reduce(jnp.maximum, peaks, top)
            mass = jnp.zeros((per_kv, 1), F32)
            mixed = jnp.zeros((per_kv, dim), F32)
            for u in range(steps):
                weight = jnp.exp(scores[u] - peak)
                mass = mass + weight
                mixed = mixed + weight * new_values[u]
            for d in range(mem_count):
                factor = jnp.exp(peaks[d] - peak)
                mass = mass + masses[d] * factor
                mixed = mixed + accum_in[d, tl, g] * factor
            own_att[tl, g * per_kv : (g + 1) * per_kv, :] = mixed / mass
    att_all[mem] = jnp.concatenate([own_att[:, h, :] for h in range(local_heads)], axis=1).astype(
        BF16
    )

    def att_copy(k, slot):
        return pltpu.make_async_remote_copy(
            att_all.at[slot],
            att_all.at[slot],
            att_send.at[k],
            att_recv.at[k],
            device_id={"mem": mem_peer(k)},
            device_id_type=MESH,
        )

    for k in range(1, mem_count):
        att_copy(k, mem).start()
    for k in range(1, mem_count):
        att_copy(k, mem_source(k)).wait_recv()
    lhs = jnp.concatenate([att_all[i].astype(F32) for i in range(mem_count)], axis=0).astype(BF16)

    def proj_copy(index, width, k, target, slot):
        view = pl.ds(index * width, width)
        return pltpu.make_async_remote_copy(
            proj.at[target, :, view],
            proj_in.at[slot, :, view],
            proj_send.at[index, k],
            proj_recv.at[index, k],
            device_id={"heads": head_peer(k)},
            device_id_type=MESH,
        )

    arrive(5)
    width = wo.shape[1] // chunks
    for index in range(chunks):
        view = pl.ds(index * width, width)
        value = jnp.dot(lhs, wo[:, view], preferred_element_type=F32)
        for owner in range(head_count):
            proj[owner, :, view] = value[owner * head_tokens : (owner + 1) * head_tokens]
        for k in range(head_count - 1, 0, -1):
            proj_copy(index, width, k, head_peer(k), head).start()
    total = proj[head]
    for k in range(1, head_count):
        for index in range(chunks):
            proj_copy(index, width, k, head_peer(k), head_source(k)).wait_recv()
        total = total + proj_in[head_source(k)]
    out_ref[...] = total.astype(BF16)

    for k in range(1, head_count):
        norm_copy(k, head).wait_send()
        for index in range(chunks):
            proj_copy(index, width, k, head_peer(k), head).wait_send()
    for k in range(1, mem_count):
        for index, start, size in pieces:
            part_copy(index, start, size, k, mem_peer(k), mem).wait_send()
        heads_copy(k, mem).wait_send()
        stat_copy(k, mem).wait_send()
        accum_copy(k, mem_peer(k), mem).wait_send()
        att_copy(k, mem).wait_send()


def shards(
    hidden,
    norm_gain,
    q_weight,
    k_weight,
    v_weight,
    o_weight,
    k_cache,
    v_cache,
    page_table,
    attend_list,
    lengths,
):
    mem_count = lax.axis_size("mem")
    head_count = lax.axis_size("heads")
    features, q_cols = q_weight.shape
    kv_cols = k_weight.shape[1]
    _, local_kv, _, dim = k_cache.shape
    row_count = lengths.shape[0]
    tokens = hidden.shape[0] * head_count
    steps = tokens // row_count
    own_tokens = tokens // mem_count
    head_tokens = hidden.shape[0]
    local_heads = q_cols // dim
    per_kv = local_heads // local_kv
    out_cols = o_weight.shape[1]
    chunks = 4
    smem = pl.BlockSpec(memory_space=pltpu.SMEM)
    vmem = pl.BlockSpec(memory_space=pltpu.VMEM)
    hbm = pl.BlockSpec(memory_space=pl.ANY)
    dma = pltpu.SemaphoreType.DMA
    total_heads = local_heads + 2 * local_kv
    return pl.pallas_call(
        functools.partial(layer_kernel, mem_count, head_count, chunks),
        out_shape=jax.ShapeDtypeStruct((head_tokens, out_cols), BF16),
        in_specs=[smem] * 3 + [vmem] * 2 + [hbm] * 6,
        out_specs=vmem,
        scratch_shapes=[
            pltpu.VMEM(q_weight.shape, BF16),
            pltpu.VMEM(k_weight.shape, BF16),
            pltpu.VMEM(v_weight.shape, BF16),
            pltpu.VMEM(o_weight.shape, BF16),
            pltpu.VMEM(k_cache.shape, BF16),
            pltpu.VMEM(v_cache.shape, BF16),
            pltpu.VMEM((head_count, head_tokens, features), BF16),
            pltpu.VMEM((mem_count, own_tokens, q_cols + 2 * kv_cols), F32),
            pltpu.VMEM((mem_count, own_tokens, q_cols + 2 * kv_cols), F32),
            pltpu.VMEM((own_tokens, total_heads, dim), F32),
            pltpu.VMEM((mem_count, own_tokens, total_heads, dim), BF16),
            pltpu.VMEM((row_count, local_kv, steps * per_kv, dim), BF16),
            pltpu.VMEM((tokens, local_kv, per_kv, dim), F32),
            pltpu.VMEM((mem_count, own_tokens, local_kv, per_kv, dim), F32),
            pltpu.VMEM((mem_count, steps, per_kv, dim), F32),
            pltpu.VMEM((own_tokens, local_heads, dim), F32),
            pltpu.VMEM((mem_count, own_tokens, q_cols), BF16),
            pltpu.VMEM((head_count, head_tokens, out_cols), F32),
            pltpu.VMEM((head_count, head_tokens, out_cols), F32),
            dma((6, PIECES)),
            dma((head_count,)),
            dma((head_count,)),
            dma((chunks + 1, mem_count)),
            dma((chunks + 1, mem_count)),
            dma((mem_count,)),
            dma((mem_count,)),
            dma((mem_count,)),
            dma((mem_count,)),
            dma((mem_count,)),
            dma((mem_count,)),
            dma((mem_count,)),
            dma((mem_count,)),
            dma((chunks, head_count)),
            dma((chunks, head_count)),
        ],
        compiler_params=pltpu.CompilerParams(
            collective_id=0, has_side_effects=True, vmem_limit_bytes=60 * 1024 * 1024
        ),
    )(
        page_table,
        attend_list,
        lengths,
        hidden,
        norm_gain.reshape(1, -1),
        q_weight,
        k_weight,
        v_weight,
        o_weight,
        k_cache,
        v_cache,
    )


def solution(mesh):
    in_specs = (
        P(("groups", "heads"), None),
        P("mem"),
        P("mem", "heads"),
        P("mem", "heads"),
        P("mem", "heads"),
        P("heads", "mem"),
        P(("groups", "mem"), "heads", None, None),
        P(("groups", "mem"), "heads", None, None),
        P("groups", None),
        P("groups", None),
        P("groups"),
    )
    out_specs = P(("groups", "heads"), "mem")
    return jax.shard_map(shards, mesh=mesh, in_specs=in_specs, out_specs=out_specs, check_vma=False)
```

```python
import functools

import jax
import jax.numpy as jnp
from jax import lax
from jax.experimental import pallas as pl
from jax.experimental.pallas import tpu as pltpu
from jax.sharding import PartitionSpec as P

MESH = pl.DeviceIdType.MESH
NEG_FILL = -1e30
EPSILON = 1e-05
PIECES = 4
F32 = jnp.float32
BF16 = jnp.bfloat16


def layer_kernel(
    mem_count,
    head_count,
    chunks,
    page_ref,
    attend_ref,
    length_ref,
    hidden_ref,
    gain_ref,
    wq_hbm,
    wk_hbm,
    wv_hbm,
    wo_hbm,
    kc_hbm,
    vc_hbm,
    out_ref,
    wq,
    wk,
    wv,
    wo,
    kc,
    vc,
    norm_buf,
    part,
    part_in,
    own_heads,
    heads_all,
    row_queries,
    accum,
    accum_in,
    stat_in,
    own_att,
    att_all,
    proj,
    proj_in,
    load_sem,
    norm_send,
    norm_recv,
    part_send,
    part_recv,
    heads_send,
    heads_recv,
    accum_send,
    accum_recv,
    stat_send,
    stat_recv,
    att_send,
    att_recv,
    proj_send,
    proj_recv,
):
    mem = lax.axis_index("mem")
    head = lax.axis_index("heads")
    row_count, sel = attend_ref.shape
    features = wq.shape[0]
    q_cols, kv_cols = wq.shape[1], wk.shape[1]
    pool, local_kv, block, dim = kc.shape
    tokens = accum.shape[0]
    steps = tokens // row_count
    own_tokens = tokens // mem_count
    head_tokens = tokens // head_count
    local_heads = q_cols // dim
    per_kv = local_heads // local_kv
    queries = steps * per_kv
    scale = dim ** (-0.5)

    def mem_peer(k):
        return lax.rem(mem + k, mem_count)

    def mem_source(k):
        return lax.rem(mem + mem_count - k, mem_count)

    def head_peer(k):
        return lax.rem(head + k, head_count)

    def head_source(k):
        return lax.rem(head + head_count - k, head_count)

    loads = []
    for which, (source, target) in enumerate(
        ((wk_hbm, wk), (wv_hbm, wv), (wq_hbm, wq), (kc_hbm, kc), (vc_hbm, vc), (wo_hbm, wo))
    ):
        rows = source.shape[0] // PIECES
        group = []
        for piece in range(PIECES):
            view = pl.ds(piece * rows, rows)
            copy = pltpu.make_async_copy(
                source.at[view], target.at[view], load_sem.at[which, piece]
            )
            group.append(copy)
        loads.append(group)

    def begin(which):
        for copy in loads[which]:
            copy.start()

    def arrive(which):
        for copy in loads[which]:
            copy.wait()

    for which in range(3):
        begin(which)
    barrier = pltpu.get_barrier_semaphore()
    for k in range(1, mem_count):
        pl.semaphore_signal(barrier, inc=1, device_id={"mem": mem_peer(k)}, device_id_type=MESH)
    for k in range(1, head_count):
        pl.semaphore_signal(barrier, inc=1, device_id={"heads": head_peer(k)}, device_id_type=MESH)

    hidden = hidden_ref[...].astype(F32)
    mean_sq = jnp.mean(hidden * hidden, axis=-1, keepdims=True)
    own = hidden_ref[:, pl.ds(pl.multiple_of(mem * features, 128), features)].astype(F32)
    normed = own * lax.rsqrt(mean_sq + EPSILON) * gain_ref[...].astype(F32).reshape(1, features)
    norm_buf[head] = normed.astype(BF16)

    pl.semaphore_wait(barrier, mem_count + head_count - 2)

    def norm_copy(k, slot):
        return pltpu.make_async_remote_copy(
            norm_buf.at[slot],
            norm_buf.at[slot],
            norm_send.at[k],
            norm_recv.at[k],
            device_id={"heads": head_peer(k)},
            device_id_type=MESH,
        )

    for k in range(head_count - 1, 0, -1):
        norm_copy(k, head).start()
    for k in range(1, head_count):
        norm_copy(k, head_source(k)).wait_recv()
    lhs = jnp.concatenate([norm_buf[i].astype(F32) for i in range(head_count)], axis=0).astype(BF16)

    def part_copy(index, start, width, k, target, slot):
        view = pl.ds(start, width)
        return pltpu.make_async_remote_copy(
            part.at[target, :, view],
            part_in.at[slot, :, view],
            part_send.at[index, k],
            part_recv.at[index, k],
            device_id={"mem": mem_peer(k)},
            device_id_type=MESH,
        )

    chunk = q_cols // chunks
    pieces = [(index, index * chunk, chunk) for index in range(chunks)]
    pieces.append((chunks, q_cols, 2 * kv_cols))

    arrive(0)
    arrive(1)
    fresh = jnp.concatenate(
        [
            jnp.dot(lhs, wk[...], preferred_element_type=F32),
            jnp.dot(lhs, wv[...], preferred_element_type=F32),
        ],
        axis=1,
    )
    for owner in range(mem_count):
        part[owner, :, q_cols:] = fresh[owner * own_tokens : (owner + 1) * own_tokens]
    for k in range(1, mem_count):
        part_copy(chunks, q_cols, 2 * kv_cols, k, mem_peer(k), mem).start()
    arrive(2)
    for which in range(3, 6):
        begin(which)
    for index, start, width in pieces[:-1]:
        view = pl.ds(start, width)
        value = jnp.dot(lhs, wq[:, view], preferred_element_type=F32)
        for owner in range(mem_count):
            part[owner, :, view] = value[owner * own_tokens : (owner + 1) * own_tokens]
        for k in range(1, mem_count):
            part_copy(index, start, width, k, mem_peer(k), mem).start()

    total = part[mem]
    for k in range(1, mem_count):
        for index, start, width in pieces:
            part_copy(index, start, width, k, mem_peer(k), mem_source(k)).wait_recv()
        total = total + part_in[mem_source(k)]
    all_heads = local_heads + 2 * local_kv
    for h in range(all_heads):
        own_heads[:, h, :] = total[:, h * dim : (h + 1) * dim]
    heads_all[mem] = own_heads[...].astype(BF16)

    def heads_copy(k, slot):
        return pltpu.make_async_remote_copy(
            heads_all.at[slot],
            heads_all.at[slot],
            heads_send.at[k],
            heads_recv.at[k],
            device_id={"mem": mem_peer(k)},
            device_id_type=MESH,
        )

    for k in range(1, mem_count):
        heads_copy(k, mem).start()
    for k in range(1, mem_count):
        heads_copy(k, mem_source(k)).wait_recv()

    for r in range(row_count):
        token_heads = []
        for s in range(steps):
            t = r * steps + s
            token_heads.append(heads_all[t // own_tokens, t % own_tokens].astype(F32))
        for g in range(local_kv):
            row_queries[r, g] = jnp.concatenate(
                [value[g * per_kv : (g + 1) * per_kv] for value in token_heads], axis=0
            ).astype(BF16)

    arrive(3)
    arrive(4)
    lane = lax.broadcasted_iota(jnp.int32, (queries, dim), 1)
    key_lane = lax.broadcasted_iota(jnp.int32, (queries, block), 1)

    def attend_row(r, stat):
        slots, counts = [], []
        for j in range(sel):
            named = attend_ref[r, j]
            slot = page_ref[r, named] - mem * pool
            local = (slot >= 0) & (slot < pool)
            slots.append(jnp.clip(slot, 0, pool - 1))
            counts.append(jnp.where(local, length_ref[r] - named * block, 0))
        for g in range(local_kv):
            keys = jnp.concatenate([kc[slot, g] for slot in slots], axis=0)
            scores = lax.dot_general(
                row_queries[r, g],
                keys,
                (((1,), (1,)), ((), ())),
                preferred_element_type=F32,
            )
            valid = [key_lane < count for count in counts]
            kept = [
                jnp.where(valid[j], scores[:, j * block : (j + 1) * block] * scale, NEG_FILL)
                for j in range(sel)
            ]
            peak = jnp.max(functools.reduce(jnp.maximum, kept), axis=1, keepdims=True)
            weights = [jnp.where(valid[j], jnp.exp(kept[j] - peak), 0.0) for j in range(sel)]
            mass = jnp.sum(functools.reduce(jnp.add, weights), axis=1, keepdims=True)
            high = [w.astype(BF16) for w in weights]
            low = [(w - h.astype(F32)).astype(BF16) for w, h in zip(weights, high)]
            both = jnp.concatenate(
                [jnp.concatenate(high, axis=1), jnp.concatenate(low, axis=1)], axis=0
            )
            values = jnp.concatenate([vc[slot, g] for slot in slots], axis=0)
            mixed = jnp.dot(both, values, preferred_element_type=F32)
            mixed = mixed[:queries] + mixed[queries:]
            for s in range(steps):
                accum[r * steps + s, g] = mixed[s * per_kv : (s + 1) * per_kv]
            spot = r * local_kv + g
            stat = jnp.where(lane == spot, peak, stat)
            stat = jnp.where(lane == spot + row_count * local_kv, mass, stat)
        return stat

    def accum_copy(k, target, slot):
        return pltpu.make_async_remote_copy(
            accum.at[pl.ds(target * own_tokens, own_tokens)],
            accum_in.at[slot],
            accum_send.at[k],
            accum_recv.at[k],
            device_id={"mem": mem_peer(k)},
            device_id_type=MESH,
        )

    stat = jnp.zeros((queries, dim), F32)
    if own_tokens % steps == 0:
        own_rows = own_tokens // steps

        def attend_owner(b, stat):
            owner = mem_peer(b + 1)
            for row in range(own_rows):
                stat = attend_row(owner * own_rows + row, stat)

            @pl.when(b < mem_count - 1)
            def _():
                accum_copy(b + 1, owner, mem).start()

            return stat

        stat = lax.fori_loop(0, mem_count, attend_owner, stat)
    else:
        stat = lax.fori_loop(0, row_count, attend_row, stat)
        for k in range(1, mem_count):
            accum_copy(k, mem_peer(k), mem).start()
    for s in range(steps):
        stat_in[mem, s] = stat[s * per_kv : (s + 1) * per_kv]

    def stat_copy(k, slot):
        return pltpu.make_async_remote_copy(
            stat_in.at[slot],
            stat_in.at[slot],
            stat_send.at[k],
            stat_recv.at[k],
            device_id={"mem": mem_peer(k)},
            device_id_type=MESH,
        )

    for k in range(1, mem_count):
        stat_copy(k, mem).start()
    accum_in[mem] = accum[pl.ds(mem * own_tokens, own_tokens)]

    fresh_parts = []
    stat_lane = lax.broadcasted_iota(jnp.int32, (per_kv, dim), 1)
    for tl in range(own_tokens):
        t = mem * own_tokens + tl
        r, s = t // steps, t % steps
        own_query = heads_all[mem, tl].astype(F32)
        row_heads = []
        for u in range(steps):
            tu = r * steps + u
            row_heads.append(heads_all[tu // own_tokens, tu % own_tokens].astype(F32))
        for g in range(local_kv):
            query = own_query[g * per_kv : (g + 1) * per_kv]
            scores, new_values = [], []
            for u in range(steps):
                at = local_heads + g
                key = row_heads[u][at : at + 1]
                at = local_heads + local_kv + g
                new_values.append(row_heads[u][at : at + 1])
                score = jnp.sum(query * key, axis=1, keepdims=True) * scale
                seen = jnp.broadcast_to(s, (per_kv, 1)) >= u
                scores.append(jnp.where(seen, score, NEG_FILL))
            top = functools.reduce(jnp.maximum, scores)
            fresh_parts.append((r, s, scores, top, new_values))

    for k in range(1, mem_count):
        stat_copy(k, mem_source(k)).wait_recv()
        accum_copy(k, mem_peer(k), mem_source(k)).wait_recv()

    for tl in range(own_tokens):
        for g in range(local_kv):
            r, s, scores, top, new_values = fresh_parts[tl * local_kv + g]
            spot = r * local_kv + g
            stats = [stat_in[d, s] for d in range(mem_count)]
            peaks = [
                jnp.sum(jnp.where(stat_lane == spot, x, 0.0), axis=1, keepdims=True) for x in stats
            ]
            masses = [
                jnp.sum(
                    jnp.where(stat_lane == spot + row_count * local_kv, x, 0.0),
                    axis=1,
                    keepdims=True,
                )
                for x in stats
            ]
            peak = functools.reduce(jnp.maximum, peaks, top)
            mass = jnp.zeros((per_kv, 1), F32)
            mixed = jnp.zeros((per_kv, dim), F32)
            for u in range(steps):
                weight = jnp.exp(scores[u] - peak)
                mass = mass + weight
                mixed = mixed + weight * new_values[u]
            for d in range(mem_count):
                factor = jnp.exp(peaks[d] - peak)
                mass = mass + masses[d] * factor
                mixed = mixed + accum_in[d, tl, g] * factor
            own_att[tl, g * per_kv : (g + 1) * per_kv, :] = mixed / mass
    att_all[mem] = jnp.concatenate([own_att[:, h, :] for h in range(local_heads)], axis=1).astype(
        BF16
    )

    def att_copy(k, slot):
        return pltpu.make_async_remote_copy(
            att_all.at[slot],
            att_all.at[slot],
            att_send.at[k],
            att_recv.at[k],
            device_id={"mem": mem_peer(k)},
            device_id_type=MESH,
        )

    for k in range(1, mem_count):
        att_copy(k, mem).start()
    for k in range(1, mem_count):
        att_copy(k, mem_source(k)).wait_recv()
    lhs = jnp.concatenate([att_all[i].astype(F32) for i in range(mem_count)], axis=0).astype(BF16)

    def proj_copy(index, width, k, target, slot):
        view = pl.ds(index * width, width)
        return pltpu.make_async_remote_copy(
            proj.at[target, :, view],
            proj_in.at[slot, :, view],
            proj_send.at[index, k],
            proj_recv.at[index, k],
            device_id={"heads": head_peer(k)},
            device_id_type=MESH,
        )

    arrive(5)
    width = wo.shape[1] // chunks
    for index in range(chunks):
        view = pl.ds(index * width, width)
        value = jnp.dot(lhs, wo[:, view], preferred_element_type=F32)
        for owner in range(head_count):
            proj[owner, :, view] = value[owner * head_tokens : (owner + 1) * head_tokens]
        for k in range(head_count - 1, 0, -1):
            proj_copy(index, width, k, head_peer(k), head).start()
    total = proj[head]
    for k in range(1, head_count):
        for index in range(chunks):
            proj_copy(index, width, k, head_peer(k), head_source(k)).wait_recv()
        total = total + proj_in[head_source(k)]
    out_ref[...] = total.astype(BF16)

    for k in range(1, head_count):
        norm_copy(k, head).wait_send()
        for index in range(chunks):
            proj_copy(index, width, k, head_peer(k), head).wait_send()
    for k in range(1, mem_count):
        for index, start, size in pieces:
            part_copy(index, start, size, k, mem_peer(k), mem).wait_send()
        heads_copy(k, mem).wait_send()
        stat_copy(k, mem).wait_send()
        accum_copy(k, mem_peer(k), mem).wait_send()
        att_copy(k, mem).wait_send()


def shards(
    hidden,
    norm_gain,
    q_weight,
    k_weight,
    v_weight,
    o_weight,
    k_cache,
    v_cache,
    page_table,
    attend_list,
    lengths,
):
    mem_count = lax.axis_size("mem")
    head_count = lax.axis_size("heads")
    features, q_cols = q_weight.shape
    kv_cols = k_weight.shape[1]
    _, local_kv, _, dim = k_cache.shape
    row_count = lengths.shape[0]
    tokens = hidden.shape[0] * head_count
    steps = tokens // row_count
    own_tokens = tokens // mem_count
    head_tokens = hidden.shape[0]
    local_heads = q_cols // dim
    per_kv = local_heads // local_kv
    out_cols = o_weight.shape[1]
    chunks = 4
    smem = pl.BlockSpec(memory_space=pltpu.SMEM)
    vmem = pl.BlockSpec(memory_space=pltpu.VMEM)
    hbm = pl.BlockSpec(memory_space=pl.ANY)
    dma = pltpu.SemaphoreType.DMA
    total_heads = local_heads + 2 * local_kv
    return pl.pallas_call(
        functools.partial(layer_kernel, mem_count, head_count, chunks),
        out_shape=jax.ShapeDtypeStruct((head_tokens, out_cols), BF16),
        in_specs=[smem] * 3 + [vmem] * 2 + [hbm] * 6,
        out_specs=vmem,
        scratch_shapes=[
            pltpu.VMEM(q_weight.shape, BF16),
            pltpu.VMEM(k_weight.shape, BF16),
            pltpu.VMEM(v_weight.shape, BF16),
            pltpu.VMEM(o_weight.shape, BF16),
            pltpu.VMEM(k_cache.shape, BF16),
            pltpu.VMEM(v_cache.shape, BF16),
            pltpu.VMEM((head_count, head_tokens, features), BF16),
            pltpu.VMEM((mem_count, own_tokens, q_cols + 2 * kv_cols), F32),
            pltpu.VMEM((mem_count, own_tokens, q_cols + 2 * kv_cols), F32),
            pltpu.VMEM((own_tokens, total_heads, dim), F32),
            pltpu.VMEM((mem_count, own_tokens, total_heads, dim), BF16),
            pltpu.VMEM((row_count, local_kv, steps * per_kv, dim), BF16),
            pltpu.VMEM((tokens, local_kv, per_kv, dim), F32),
            pltpu.VMEM((mem_count, own_tokens, local_kv, per_kv, dim), F32),
            pltpu.VMEM((mem_count, steps, per_kv, dim), F32),
            pltpu.VMEM((own_tokens, local_heads, dim), F32),
            pltpu.VMEM((mem_count, own_tokens, q_cols), BF16),
            pltpu.VMEM((head_count, head_tokens, out_cols), F32),
            pltpu.VMEM((head_count, head_tokens, out_cols), F32),
            dma((6, PIECES)),
            dma((head_count,)),
            dma((head_count,)),
            dma((chunks + 1, mem_count)),
            dma((chunks + 1, mem_count)),
            dma((mem_count,)),
            dma((mem_count,)),
            dma((mem_count,)),
            dma((mem_count,)),
            dma((mem_count,)),
            dma((mem_count,)),
            dma((mem_count,)),
            dma((mem_count,)),
            dma((chunks, head_count)),
            dma((chunks, head_count)),
        ],
        compiler_params=pltpu.CompilerParams(
            collective_id=0, has_side_effects=True, vmem_limit_bytes=60 * 1024 * 1024
        ),
    )(
        page_table,
        attend_list,
        lengths,
        hidden,
        norm_gain,
        q_weight,
        k_weight,
        v_weight,
        o_weight,
        k_cache,
        v_cache,
    )


def solution(mesh):
    in_specs = (
        P(("groups", "heads"), None),
        P("mem"),
        P("mem", "heads"),
        P("mem", "heads"),
        P("mem", "heads"),
        P("heads", "mem"),
        P(("groups", "mem"), "heads", None, None),
        P(("groups", "mem"), "heads", None, None),
        P("groups", None),
        P("groups", None),
        P("groups"),
    )
    out_specs = P(("groups", "heads"), "mem")
    return jax.shard_map(shards, mesh=mesh, in_specs=in_specs, out_specs=out_specs, check_vma=False)
```

```python
import functools

import jax
import jax.numpy as jnp
from jax import lax
from jax.experimental import pallas as pl
from jax.experimental.pallas import tpu as pltpu
from jax.sharding import PartitionSpec as P

MESH = pl.DeviceIdType.MESH
NEG_FILL = -1e30
EPSILON = 1e-05
PIECES = 4
F32 = jnp.float32
BF16 = jnp.bfloat16


def layer_kernel(
    mem_count,
    head_count,
    chunks,
    page_ref,
    attend_ref,
    length_ref,
    hidden_ref,
    gain_ref,
    wq_hbm,
    wk_hbm,
    wv_hbm,
    wo_hbm,
    kc_hbm,
    vc_hbm,
    out_ref,
    wq,
    wk,
    wv,
    wo,
    kc,
    vc,
    norm_buf,
    part,
    part_in,
    own_heads,
    heads_all,
    row_queries,
    accum,
    accum_in,
    stat_in,
    own_att,
    att_all,
    proj,
    proj_in,
    load_sem,
    norm_send,
    norm_recv,
    part_send,
    part_recv,
    heads_send,
    heads_recv,
    accum_send,
    accum_recv,
    stat_send,
    stat_recv,
    att_send,
    att_recv,
    proj_send,
    proj_recv,
):
    mem = lax.axis_index("mem")
    head = lax.axis_index("heads")
    row_count, sel = attend_ref.shape
    features = wq.shape[0]
    q_cols, kv_cols = wq.shape[1], wk.shape[1]
    pool, local_kv, block, dim = kc.shape
    tokens = accum.shape[0]
    steps = tokens // row_count
    own_tokens = tokens // mem_count
    head_tokens = tokens // head_count
    local_heads = q_cols // dim
    per_kv = local_heads // local_kv
    queries = steps * per_kv
    scale = dim ** (-0.5)

    def mem_peer(k):
        return lax.rem(mem + k, mem_count)

    def mem_source(k):
        return lax.rem(mem + mem_count - k, mem_count)

    def head_peer(k):
        return lax.rem(head + k, head_count)

    def head_source(k):
        return lax.rem(head + head_count - k, head_count)

    loads = []
    for which, (source, target) in enumerate(
        ((wk_hbm, wk), (wv_hbm, wv), (wq_hbm, wq), (kc_hbm, kc), (vc_hbm, vc), (wo_hbm, wo))
    ):
        rows = source.shape[0] // PIECES
        group = []
        for piece in range(PIECES):
            view = pl.ds(piece * rows, rows)
            copy = pltpu.make_async_copy(
                source.at[view], target.at[view], load_sem.at[which, piece]
            )
            group.append(copy)
        loads.append(group)

    def begin(which):
        for copy in loads[which]:
            copy.start()

    def arrive(which):
        for copy in loads[which]:
            copy.wait()

    for which in range(3):
        begin(which)
    barrier = pltpu.get_barrier_semaphore()
    for k in range(1, mem_count):
        pl.semaphore_signal(barrier, inc=1, device_id={"mem": mem_peer(k)}, device_id_type=MESH)
    for k in range(1, head_count):
        pl.semaphore_signal(barrier, inc=1, device_id={"heads": head_peer(k)}, device_id_type=MESH)

    hidden = hidden_ref[...].astype(F32)
    mean_sq = jnp.mean(hidden * hidden, axis=-1, keepdims=True)
    own = hidden_ref[:, pl.ds(pl.multiple_of(mem * features, 128), features)].astype(F32)
    normed = own * lax.rsqrt(mean_sq + EPSILON) * gain_ref[...].astype(F32).reshape(1, features)
    norm_buf[head] = normed.astype(BF16)

    pl.semaphore_wait(barrier, mem_count + head_count - 2)

    def norm_copy(k, slot):
        return pltpu.make_async_remote_copy(
            norm_buf.at[slot],
            norm_buf.at[slot],
            norm_send.at[k],
            norm_recv.at[k],
            device_id={"heads": head_peer(k)},
            device_id_type=MESH,
        )

    for k in range(head_count - 1, 0, -1):
        norm_copy(k, head).start()
    for k in range(1, head_count):
        norm_copy(k, head_source(k)).wait_recv()
    lhs = jnp.concatenate([norm_buf[i].astype(F32) for i in range(head_count)], axis=0).astype(BF16)

    def part_copy(index, start, width, k, target, slot):
        view = pl.ds(start, width)
        return pltpu.make_async_remote_copy(
            part.at[target, :, view],
            part_in.at[slot, :, view],
            part_send.at[index, k],
            part_recv.at[index, k],
            device_id={"mem": mem_peer(k)},
            device_id_type=MESH,
        )

    chunk = q_cols // chunks
    pieces = [(index, index * chunk, chunk) for index in range(chunks)]
    pieces.append((chunks, q_cols, 2 * kv_cols))

    arrive(0)
    arrive(1)
    fresh = jnp.concatenate(
        [
            jnp.dot(lhs, wk[...], preferred_element_type=F32),
            jnp.dot(lhs, wv[...], preferred_element_type=F32),
        ],
        axis=1,
    )
    for owner in range(mem_count):
        part[owner, :, q_cols:] = fresh[owner * own_tokens : (owner + 1) * own_tokens]
    for k in range(1, mem_count):
        part_copy(chunks, q_cols, 2 * kv_cols, k, mem_peer(k), mem).start()
    arrive(2)
    for which in range(3, 6):
        begin(which)
    for index, start, width in pieces[:-1]:
        view = pl.ds(start, width)
        value = jnp.dot(lhs, wq[:, view], preferred_element_type=F32)
        for owner in range(mem_count):
            part[owner, :, view] = value[owner * own_tokens : (owner + 1) * own_tokens]
        for k in range(1, mem_count):
            part_copy(index, start, width, k, mem_peer(k), mem).start()

    total = part[mem]
    for k in range(1, mem_count):
        for index, start, width in pieces:
            part_copy(index, start, width, k, mem_peer(k), mem_source(k)).wait_recv()
        total = total + part_in[mem_source(k)]
    all_heads = local_heads + 2 * local_kv
    for h in range(all_heads):
        own_heads[:, h, :] = total[:, h * dim : (h + 1) * dim]
    heads_all[mem] = own_heads[...].astype(BF16)

    def heads_copy(k, slot):
        return pltpu.make_async_remote_copy(
            heads_all.at[slot],
            heads_all.at[slot],
            heads_send.at[k],
            heads_recv.at[k],
            device_id={"mem": mem_peer(k)},
            device_id_type=MESH,
        )

    for k in range(1, mem_count):
        heads_copy(k, mem).start()
    for k in range(1, mem_count):
        heads_copy(k, mem_source(k)).wait_recv()

    for r in range(row_count):
        token_heads = []
        for s in range(steps):
            t = r * steps + s
            token_heads.append(heads_all[t // own_tokens, t % own_tokens].astype(F32))
        for g in range(local_kv):
            row_queries[r, g] = jnp.concatenate(
                [value[g * per_kv : (g + 1) * per_kv] for value in token_heads], axis=0
            ).astype(BF16)

    arrive(3)
    arrive(4)
    lane = lax.broadcasted_iota(jnp.int32, (queries, dim), 1)
    key_lane = lax.broadcasted_iota(jnp.int32, (queries, block), 1)

    def attend_rows(rows, stat):
        jobs, masks, slot_lists = [], {}, {}
        for n, r in enumerate(rows):
            slots, masks[n] = [], []
            for j in range(sel):
                named = attend_ref[r, j]
                slot = page_ref[r, named] - mem * pool
                local = (slot >= 0) & (slot < pool)
                slots.append(jnp.clip(slot, 0, pool - 1))
                masks[n].append(key_lane < jnp.where(local, length_ref[r] - named * block, 0))
            slot_lists[n] = slots
            jobs.extend((n, r, g) for g in range(local_kv))
        raw = [
            lax.dot_general(
                row_queries[r, g],
                jnp.concatenate([kc[slot, g] for slot in slot_lists[n]], axis=0),
                (((1,), (1,)), ((), ())),
                preferred_element_type=F32,
            )
            for n, r, g in jobs
        ]
        kept = [
            [
                jnp.where(masks[n][j], scores[:, j * block : (j + 1) * block] * scale, NEG_FILL)
                for j in range(sel)
            ]
            for (n, r, g), scores in zip(jobs, raw)
        ]
        peaks = [
            jnp.max(functools.reduce(jnp.maximum, x), axis=1, keepdims=True) for x in kept
        ]
        weights = [
            [jnp.where(masks[n][j], jnp.exp(x[j] - peak), 0.0) for j in range(sel)]
            for (n, r, g), x, peak in zip(jobs, kept, peaks)
        ]
        masses = [
            jnp.sum(functools.reduce(jnp.add, x), axis=1, keepdims=True) for x in weights
        ]
        outs = []
        for (n, r, g), x in zip(jobs, weights):
            high = [w.astype(BF16) for w in x]
            low = [(w - h.astype(F32)).astype(BF16) for w, h in zip(x, high)]
            both = jnp.concatenate(
                [jnp.concatenate(high, axis=1), jnp.concatenate(low, axis=1)], axis=0
            )
            values = jnp.concatenate([vc[slot, g] for slot in slot_lists[n]], axis=0)
            outs.append(jnp.dot(both, values, preferred_element_type=F32))
        for (n, r, g), mixed, peak, mass in zip(jobs, outs, peaks, masses):
            mixed = mixed[:queries] + mixed[queries:]
            for s in range(steps):
                accum[r * steps + s, g] = mixed[s * per_kv : (s + 1) * per_kv]
            spot = r * local_kv + g
            stat = jnp.where(lane == spot, peak, stat)
            stat = jnp.where(lane == spot + row_count * local_kv, mass, stat)
        return stat

    def accum_copy(k, target, slot):
        return pltpu.make_async_remote_copy(
            accum.at[pl.ds(target * own_tokens, own_tokens)],
            accum_in.at[slot],
            accum_send.at[k],
            accum_recv.at[k],
            device_id={"mem": mem_peer(k)},
            device_id_type=MESH,
        )

    stat = jnp.zeros((queries, dim), F32)
    if own_tokens % steps == 0:
        own_rows = own_tokens // steps

        def attend_owner(b, stat):
            owner = mem_peer(b + 1)
            stat = attend_rows([owner * own_rows + row for row in range(own_rows)], stat)

            @pl.when(b < mem_count - 1)
            def _():
                accum_copy(b + 1, owner, mem).start()

            return stat

        stat = lax.fori_loop(0, mem_count, attend_owner, stat)
    else:
        stat = lax.fori_loop(0, row_count, lambda r, x: attend_rows([r], x), stat)
        for k in range(1, mem_count):
            accum_copy(k, mem_peer(k), mem).start()
    for s in range(steps):
        stat_in[mem, s] = stat[s * per_kv : (s + 1) * per_kv]

    def stat_copy(k, slot):
        return pltpu.make_async_remote_copy(
            stat_in.at[slot],
            stat_in.at[slot],
            stat_send.at[k],
            stat_recv.at[k],
            device_id={"mem": mem_peer(k)},
            device_id_type=MESH,
        )

    for k in range(1, mem_count):
        stat_copy(k, mem).start()
    accum_in[mem] = accum[pl.ds(mem * own_tokens, own_tokens)]

    fresh_parts = []
    stat_lane = lax.broadcasted_iota(jnp.int32, (per_kv, dim), 1)
    for tl in range(own_tokens):
        t = mem * own_tokens + tl
        r, s = t // steps, t % steps
        own_query = heads_all[mem, tl].astype(F32)
        row_heads = []
        for u in range(steps):
            tu = r * steps + u
            row_heads.append(heads_all[tu // own_tokens, tu % own_tokens].astype(F32))
        for g in range(local_kv):
            query = own_query[g * per_kv : (g + 1) * per_kv]
            scores, new_values = [], []
            for u in range(steps):
                at = local_heads + g
                key = row_heads[u][at : at + 1]
                at = local_heads + local_kv + g
                new_values.append(row_heads[u][at : at + 1])
                score = jnp.sum(query * key, axis=1, keepdims=True) * scale
                seen = jnp.broadcast_to(s, (per_kv, 1)) >= u
                scores.append(jnp.where(seen, score, NEG_FILL))
            top = functools.reduce(jnp.maximum, scores)
            fresh_parts.append((r, s, scores, top, new_values))

    for k in range(1, mem_count):
        stat_copy(k, mem_source(k)).wait_recv()
        accum_copy(k, mem_peer(k), mem_source(k)).wait_recv()

    for tl in range(own_tokens):
        for g in range(local_kv):
            r, s, scores, top, new_values = fresh_parts[tl * local_kv + g]
            spot = r * local_kv + g
            stats = [stat_in[d, s] for d in range(mem_count)]
            peaks = [
                jnp.sum(jnp.where(stat_lane == spot, x, 0.0), axis=1, keepdims=True) for x in stats
            ]
            masses = [
                jnp.sum(
                    jnp.where(stat_lane == spot + row_count * local_kv, x, 0.0),
                    axis=1,
                    keepdims=True,
                )
                for x in stats
            ]
            peak = functools.reduce(jnp.maximum, peaks, top)
            mass = jnp.zeros((per_kv, 1), F32)
            mixed = jnp.zeros((per_kv, dim), F32)
            for u in range(steps):
                weight = jnp.exp(scores[u] - peak)
                mass = mass + weight
                mixed = mixed + weight * new_values[u]
            for d in range(mem_count):
                factor = jnp.exp(peaks[d] - peak)
                mass = mass + masses[d] * factor
                mixed = mixed + accum_in[d, tl, g] * factor
            own_att[tl, g * per_kv : (g + 1) * per_kv, :] = mixed / mass
    att_all[mem] = jnp.concatenate([own_att[:, h, :] for h in range(local_heads)], axis=1).astype(
        BF16
    )

    def att_copy(k, slot):
        return pltpu.make_async_remote_copy(
            att_all.at[slot],
            att_all.at[slot],
            att_send.at[k],
            att_recv.at[k],
            device_id={"mem": mem_peer(k)},
            device_id_type=MESH,
        )

    for k in range(1, mem_count):
        att_copy(k, mem).start()
    for k in range(1, mem_count):
        att_copy(k, mem_source(k)).wait_recv()
    lhs = jnp.concatenate([att_all[i].astype(F32) for i in range(mem_count)], axis=0).astype(BF16)

    def proj_copy(index, width, k, target, slot):
        view = pl.ds(index * width, width)
        return pltpu.make_async_remote_copy(
            proj.at[target, :, view],
            proj_in.at[slot, :, view],
            proj_send.at[index, k],
            proj_recv.at[index, k],
            device_id={"heads": head_peer(k)},
            device_id_type=MESH,
        )

    arrive(5)
    width = wo.shape[1] // chunks
    for index in range(chunks):
        view = pl.ds(index * width, width)
        value = jnp.dot(lhs, wo[:, view], preferred_element_type=F32)
        for owner in range(head_count):
            proj[owner, :, view] = value[owner * head_tokens : (owner + 1) * head_tokens]
        for k in range(head_count - 1, 0, -1):
            proj_copy(index, width, k, head_peer(k), head).start()
    total = proj[head]
    for k in range(1, head_count):
        for index in range(chunks):
            proj_copy(index, width, k, head_peer(k), head_source(k)).wait_recv()
        total = total + proj_in[head_source(k)]
    out_ref[...] = total.astype(BF16)

    for k in range(1, head_count):
        norm_copy(k, head).wait_send()
        for index in range(chunks):
            proj_copy(index, width, k, head_peer(k), head).wait_send()
    for k in range(1, mem_count):
        for index, start, size in pieces:
            part_copy(index, start, size, k, mem_peer(k), mem).wait_send()
        heads_copy(k, mem).wait_send()
        stat_copy(k, mem).wait_send()
        accum_copy(k, mem_peer(k), mem).wait_send()
        att_copy(k, mem).wait_send()


def shards(
    hidden,
    norm_gain,
    q_weight,
    k_weight,
    v_weight,
    o_weight,
    k_cache,
    v_cache,
    page_table,
    attend_list,
    lengths,
):
    mem_count = lax.axis_size("mem")
    head_count = lax.axis_size("heads")
    features, q_cols = q_weight.shape
    kv_cols = k_weight.shape[1]
    _, local_kv, _, dim = k_cache.shape
    row_count = lengths.shape[0]
    tokens = hidden.shape[0] * head_count
    steps = tokens // row_count
    own_tokens = tokens // mem_count
    head_tokens = hidden.shape[0]
    local_heads = q_cols // dim
    per_kv = local_heads // local_kv
    out_cols = o_weight.shape[1]
    chunks = 4
    smem = pl.BlockSpec(memory_space=pltpu.SMEM)
    vmem = pl.BlockSpec(memory_space=pltpu.VMEM)
    hbm = pl.BlockSpec(memory_space=pl.ANY)
    dma = pltpu.SemaphoreType.DMA
    total_heads = local_heads + 2 * local_kv
    return pl.pallas_call(
        functools.partial(layer_kernel, mem_count, head_count, chunks),
        out_shape=jax.ShapeDtypeStruct((head_tokens, out_cols), BF16),
        in_specs=[smem] * 3 + [vmem] * 2 + [hbm] * 6,
        out_specs=vmem,
        scratch_shapes=[
            pltpu.VMEM(q_weight.shape, BF16),
            pltpu.VMEM(k_weight.shape, BF16),
            pltpu.VMEM(v_weight.shape, BF16),
            pltpu.VMEM(o_weight.shape, BF16),
            pltpu.VMEM(k_cache.shape, BF16),
            pltpu.VMEM(v_cache.shape, BF16),
            pltpu.VMEM((head_count, head_tokens, features), BF16),
            pltpu.VMEM((mem_count, own_tokens, q_cols + 2 * kv_cols), F32),
            pltpu.VMEM((mem_count, own_tokens, q_cols + 2 * kv_cols), F32),
            pltpu.VMEM((own_tokens, total_heads, dim), F32),
            pltpu.VMEM((mem_count, own_tokens, total_heads, dim), BF16),
            pltpu.VMEM((row_count, local_kv, steps * per_kv, dim), BF16),
            pltpu.VMEM((tokens, local_kv, per_kv, dim), F32),
            pltpu.VMEM((mem_count, own_tokens, local_kv, per_kv, dim), F32),
            pltpu.VMEM((mem_count, steps, per_kv, dim), F32),
            pltpu.VMEM((own_tokens, local_heads, dim), F32),
            pltpu.VMEM((mem_count, own_tokens, q_cols), BF16),
            pltpu.VMEM((head_count, head_tokens, out_cols), F32),
            pltpu.VMEM((head_count, head_tokens, out_cols), F32),
            dma((6, PIECES)),
            dma((head_count,)),
            dma((head_count,)),
            dma((chunks + 1, mem_count)),
            dma((chunks + 1, mem_count)),
            dma((mem_count,)),
            dma((mem_count,)),
            dma((mem_count,)),
            dma((mem_count,)),
            dma((mem_count,)),
            dma((mem_count,)),
            dma((mem_count,)),
            dma((mem_count,)),
            dma((chunks, head_count)),
            dma((chunks, head_count)),
        ],
        compiler_params=pltpu.CompilerParams(
            collective_id=0, has_side_effects=True, vmem_limit_bytes=60 * 1024 * 1024
        ),
    )(
        page_table,
        attend_list,
        lengths,
        hidden,
        norm_gain,
        q_weight,
        k_weight,
        v_weight,
        o_weight,
        k_cache,
        v_cache,
    )


def solution(mesh):
    in_specs = (
        P(("groups", "heads"), None),
        P("mem"),
        P("mem", "heads"),
        P("mem", "heads"),
        P("mem", "heads"),
        P("heads", "mem"),
        P(("groups", "mem"), "heads", None, None),
        P(("groups", "mem"), "heads", None, None),
        P("groups", None),
        P("groups", None),
        P("groups"),
    )
    out_specs = P(("groups", "heads"), "mem")
    return jax.shard_map(shards, mesh=mesh, in_specs=in_specs, out_specs=out_specs, check_vma=False)
```

```python
import functools

import jax
import jax.numpy as jnp
from jax import lax
from jax.experimental import pallas as pl
from jax.experimental.pallas import tpu as pltpu
from jax.sharding import PartitionSpec as P

MESH = pl.DeviceIdType.MESH
NEG_FILL = -1e30
EPSILON = 1e-05
PIECES = 4
F32 = jnp.float32
BF16 = jnp.bfloat16


def layer_kernel(
    mem_count,
    head_count,
    chunks,
    page_ref,
    attend_ref,
    length_ref,
    hidden_ref,
    gain_ref,
    wq_hbm,
    wk_hbm,
    wv_hbm,
    wo_hbm,
    kc_hbm,
    vc_hbm,
    out_ref,
    wq,
    wk,
    wv,
    wo,
    kc,
    vc,
    norm_buf,
    part,
    part_in,
    own_heads,
    heads_all,
    row_queries,
    accum,
    accum_in,
    stat_in,
    own_att,
    att_all,
    proj,
    proj_in,
    load_sem,
    norm_send,
    norm_recv,
    part_send,
    part_recv,
    heads_send,
    heads_recv,
    accum_send,
    accum_recv,
    stat_send,
    stat_recv,
    att_send,
    att_recv,
    proj_send,
    proj_recv,
):
    mem = lax.axis_index("mem")
    head = lax.axis_index("heads")
    row_count, sel = attend_ref.shape
    features = wq.shape[0]
    q_cols, kv_cols = wq.shape[1], wk.shape[1]
    pool, local_kv, block, dim = kc.shape
    tokens = accum.shape[0]
    steps = tokens // row_count
    own_tokens = tokens // mem_count
    head_tokens = tokens // head_count
    local_heads = q_cols // dim
    per_kv = local_heads // local_kv
    queries = steps * per_kv
    scale = dim ** (-0.5)

    def mem_peer(k):
        return lax.rem(mem + k, mem_count)

    def mem_source(k):
        return lax.rem(mem + mem_count - k, mem_count)

    def head_peer(k):
        return lax.rem(head + k, head_count)

    def head_source(k):
        return lax.rem(head + head_count - k, head_count)

    loads = []
    for which, (source, target) in enumerate(
        ((wk_hbm, wk), (wv_hbm, wv), (wq_hbm, wq), (kc_hbm, kc), (vc_hbm, vc), (wo_hbm, wo))
    ):
        rows = source.shape[0] // PIECES
        group = []
        for piece in range(PIECES):
            view = pl.ds(piece * rows, rows)
            copy = pltpu.make_async_copy(
                source.at[view], target.at[view], load_sem.at[which, piece]
            )
            group.append(copy)
        loads.append(group)

    def begin(which):
        for copy in loads[which]:
            copy.start()

    def arrive(which):
        for copy in loads[which]:
            copy.wait()

    for which in range(3):
        begin(which)
    barrier = pltpu.get_barrier_semaphore()
    for k in range(1, mem_count):
        pl.semaphore_signal(barrier, inc=1, device_id={"mem": mem_peer(k)}, device_id_type=MESH)
    for k in range(1, head_count):
        pl.semaphore_signal(barrier, inc=1, device_id={"heads": head_peer(k)}, device_id_type=MESH)

    hidden = hidden_ref[...].astype(F32)
    mean_sq = jnp.mean(hidden * hidden, axis=-1, keepdims=True)
    own = hidden_ref[:, pl.ds(pl.multiple_of(mem * features, 128), features)].astype(F32)
    normed = own * lax.rsqrt(mean_sq + EPSILON) * gain_ref[...].astype(F32).reshape(1, features)
    norm_buf[head] = normed.astype(BF16)

    pl.semaphore_wait(barrier, mem_count + head_count - 2)

    def norm_copy(k, slot):
        return pltpu.make_async_remote_copy(
            norm_buf.at[slot],
            norm_buf.at[slot],
            norm_send.at[k],
            norm_recv.at[k],
            device_id={"heads": head_peer(k)},
            device_id_type=MESH,
        )

    for k in range(head_count - 1, 0, -1):
        norm_copy(k, head).start()
    for k in range(1, head_count):
        norm_copy(k, head_source(k)).wait_recv()
    lhs = jnp.concatenate([norm_buf[i].astype(F32) for i in range(head_count)], axis=0).astype(BF16)

    def part_copy(index, start, width, k, target, slot):
        view = pl.ds(start, width)
        return pltpu.make_async_remote_copy(
            part.at[target, :, view],
            part_in.at[slot, :, view],
            part_send.at[index, k],
            part_recv.at[index, k],
            device_id={"mem": mem_peer(k)},
            device_id_type=MESH,
        )

    chunk = q_cols // chunks
    pieces = [(index, index * chunk, chunk) for index in range(chunks)]
    pieces.append((chunks, q_cols, 2 * kv_cols))

    arrive(0)
    arrive(1)
    fresh = jnp.concatenate(
        [
            jnp.dot(lhs, wk[...], preferred_element_type=F32),
            jnp.dot(lhs, wv[...], preferred_element_type=F32),
        ],
        axis=1,
    )
    for owner in range(mem_count):
        part[owner, :, q_cols:] = fresh[owner * own_tokens : (owner + 1) * own_tokens]
    for k in range(1, mem_count):
        part_copy(chunks, q_cols, 2 * kv_cols, k, mem_peer(k), mem).start()
    arrive(2)
    for which in range(3, 6):
        begin(which)
    for index, start, width in pieces[:-1]:
        view = pl.ds(start, width)
        value = jnp.dot(lhs, wq[:, view], preferred_element_type=F32)
        for owner in range(mem_count):
            part[owner, :, view] = value[owner * own_tokens : (owner + 1) * own_tokens]
        for k in range(1, mem_count):
            part_copy(index, start, width, k, mem_peer(k), mem).start()

    total = part[mem]
    for k in range(1, mem_count):
        for index, start, width in pieces:
            part_copy(index, start, width, k, mem_peer(k), mem_source(k)).wait_recv()
        total = total + part_in[mem_source(k)]
    all_heads = local_heads + 2 * local_kv
    for h in range(all_heads):
        own_heads[:, h, :] = total[:, h * dim : (h + 1) * dim]
    heads_all[mem] = own_heads[...].astype(BF16)

    def heads_copy(k, slot):
        return pltpu.make_async_remote_copy(
            heads_all.at[slot],
            heads_all.at[slot],
            heads_send.at[k],
            heads_recv.at[k],
            device_id={"mem": mem_peer(k)},
            device_id_type=MESH,
        )

    for k in range(1, mem_count):
        heads_copy(k, mem).start()
    for k in range(1, mem_count):
        heads_copy(k, mem_source(k)).wait_recv()

    for r in range(row_count):
        token_heads = []
        for s in range(steps):
            t = r * steps + s
            token_heads.append(heads_all[t // own_tokens, t % own_tokens].astype(F32))
        for g in range(local_kv):
            row_queries[r, g] = jnp.concatenate(
                [value[g * per_kv : (g + 1) * per_kv] for value in token_heads], axis=0
            ).astype(BF16)

    arrive(3)
    arrive(4)
    lane = lax.broadcasted_iota(jnp.int32, (queries, dim), 1)
    key_lane = lax.broadcasted_iota(jnp.int32, (queries, block), 1)

    def attend_rows(rows, stat):
        jobs, masks, slot_lists = [], {}, {}
        for n, r in enumerate(rows):
            slots, masks[n] = [], []
            for j in range(sel):
                named = attend_ref[r, j]
                slot = page_ref[r, named] - mem * pool
                local = (slot >= 0) & (slot < pool)
                slots.append(jnp.clip(slot, 0, pool - 1))
                masks[n].append(key_lane < jnp.where(local, length_ref[r] - named * block, 0))
            slot_lists[n] = slots
            jobs.extend((n, r, g) for g in range(local_kv))
        raw = [
            lax.dot_general(
                row_queries[r, g],
                jnp.concatenate([kc[slot, g] for slot in slot_lists[n]], axis=0),
                (((1,), (1,)), ((), ())),
                preferred_element_type=F32,
            )
            for n, r, g in jobs
        ]
        kept = [
            [
                jnp.where(masks[n][j], scores[:, j * block : (j + 1) * block] * scale, NEG_FILL)
                for j in range(sel)
            ]
            for (n, r, g), scores in zip(jobs, raw)
        ]
        peaks = [
            jnp.max(functools.reduce(jnp.maximum, x), axis=1, keepdims=True) for x in kept
        ]
        weights = [
            [jnp.where(masks[n][j], jnp.exp(x[j] - peak), 0.0) for j in range(sel)]
            for (n, r, g), x, peak in zip(jobs, kept, peaks)
        ]
        masses = [
            jnp.sum(functools.reduce(jnp.add, x), axis=1, keepdims=True) for x in weights
        ]
        outs = []
        for (n, r, g), x in zip(jobs, weights):
            high = [w.astype(BF16) for w in x]
            low = [(w - h.astype(F32)).astype(BF16) for w, h in zip(x, high)]
            both = jnp.concatenate(
                [jnp.concatenate(high, axis=1), jnp.concatenate(low, axis=1)], axis=0
            )
            values = jnp.concatenate([vc[slot, g] for slot in slot_lists[n]], axis=0)
            outs.append(jnp.dot(both, values, preferred_element_type=F32))
        for (n, r, g), mixed, peak, mass in zip(jobs, outs, peaks, masses):
            mixed = mixed[:queries] + mixed[queries:]
            for s in range(steps):
                accum[r * steps + s, g] = mixed[s * per_kv : (s + 1) * per_kv]
            spot = r * local_kv + g
            stat = jnp.where(lane == spot, peak, stat)
            stat = jnp.where(lane == spot + row_count * local_kv, mass, stat)
        return stat

    def accum_copy(k, target, slot):
        return pltpu.make_async_remote_copy(
            accum.at[pl.ds(target * own_tokens, own_tokens)],
            accum_in.at[slot],
            accum_send.at[k],
            accum_recv.at[k],
            device_id={"mem": mem_peer(k)},
            device_id_type=MESH,
        )

    stat = jnp.zeros((queries, dim), F32)
    if own_tokens % steps == 0:
        own_rows = own_tokens // steps

        together = 2 if mem_count % 2 == 0 else 1

        def attend_owners(b, stat):
            first = b * together + 1
            owners = [mem_peer(first + i) for i in range(together)]
            rows = [owner * own_rows + row for owner in owners for row in range(own_rows)]
            stat = attend_rows(rows, stat)
            for i, owner in enumerate(owners):

                @pl.when(first + i < mem_count)
                def _():
                    accum_copy(first + i, owner, mem).start()

            return stat

        stat = lax.fori_loop(0, mem_count // together, attend_owners, stat)
    else:
        stat = lax.fori_loop(0, row_count, lambda r, x: attend_rows([r], x), stat)
        for k in range(1, mem_count):
            accum_copy(k, mem_peer(k), mem).start()
    for s in range(steps):
        stat_in[mem, s] = stat[s * per_kv : (s + 1) * per_kv]

    def stat_copy(k, slot):
        return pltpu.make_async_remote_copy(
            stat_in.at[slot],
            stat_in.at[slot],
            stat_send.at[k],
            stat_recv.at[k],
            device_id={"mem": mem_peer(k)},
            device_id_type=MESH,
        )

    for k in range(1, mem_count):
        stat_copy(k, mem).start()
    accum_in[mem] = accum[pl.ds(mem * own_tokens, own_tokens)]

    fresh_parts = []
    stat_lane = lax.broadcasted_iota(jnp.int32, (per_kv, dim), 1)
    for tl in range(own_tokens):
        t = mem * own_tokens + tl
        r, s = t // steps, t % steps
        own_query = heads_all[mem, tl].astype(F32)
        row_heads = []
        for u in range(steps):
            tu = r * steps + u
            row_heads.append(heads_all[tu // own_tokens, tu % own_tokens].astype(F32))
        for g in range(local_kv):
            query = own_query[g * per_kv : (g + 1) * per_kv]
            scores, new_values = [], []
            for u in range(steps):
                at = local_heads + g
                key = row_heads[u][at : at + 1]
                at = local_heads + local_kv + g
                new_values.append(row_heads[u][at : at + 1])
                score = jnp.sum(query * key, axis=1, keepdims=True) * scale
                seen = jnp.broadcast_to(s, (per_kv, 1)) >= u
                scores.append(jnp.where(seen, score, NEG_FILL))
            top = functools.reduce(jnp.maximum, scores)
            fresh_parts.append((r, s, scores, top, new_values))

    for k in range(1, mem_count):
        stat_copy(k, mem_source(k)).wait_recv()
        accum_copy(k, mem_peer(k), mem_source(k)).wait_recv()

    for tl in range(own_tokens):
        for g in range(local_kv):
            r, s, scores, top, new_values = fresh_parts[tl * local_kv + g]
            spot = r * local_kv + g
            stats = [stat_in[d, s] for d in range(mem_count)]
            peaks = [
                jnp.sum(jnp.where(stat_lane == spot, x, 0.0), axis=1, keepdims=True) for x in stats
            ]
            masses = [
                jnp.sum(
                    jnp.where(stat_lane == spot + row_count * local_kv, x, 0.0),
                    axis=1,
                    keepdims=True,
                )
                for x in stats
            ]
            peak = functools.reduce(jnp.maximum, peaks, top)
            mass = jnp.zeros((per_kv, 1), F32)
            mixed = jnp.zeros((per_kv, dim), F32)
            for u in range(steps):
                weight = jnp.exp(scores[u] - peak)
                mass = mass + weight
                mixed = mixed + weight * new_values[u]
            for d in range(mem_count):
                factor = jnp.exp(peaks[d] - peak)
                mass = mass + masses[d] * factor
                mixed = mixed + accum_in[d, tl, g] * factor
            own_att[tl, g * per_kv : (g + 1) * per_kv, :] = mixed / mass
    att_all[mem] = jnp.concatenate([own_att[:, h, :] for h in range(local_heads)], axis=1).astype(
        BF16
    )

    def att_copy(k, slot):
        return pltpu.make_async_remote_copy(
            att_all.at[slot],
            att_all.at[slot],
            att_send.at[k],
            att_recv.at[k],
            device_id={"mem": mem_peer(k)},
            device_id_type=MESH,
        )

    for k in range(1, mem_count):
        att_copy(k, mem).start()
    for k in range(1, mem_count):
        att_copy(k, mem_source(k)).wait_recv()
    lhs = jnp.concatenate([att_all[i].astype(F32) for i in range(mem_count)], axis=0).astype(BF16)

    def proj_copy(index, width, k, target, slot):
        view = pl.ds(index * width, width)
        return pltpu.make_async_remote_copy(
            proj.at[target, :, view],
            proj_in.at[slot, :, view],
            proj_send.at[index, k],
            proj_recv.at[index, k],
            device_id={"heads": head_peer(k)},
            device_id_type=MESH,
        )

    arrive(5)
    width = wo.shape[1] // chunks
    for index in range(chunks):
        view = pl.ds(index * width, width)
        value = jnp.dot(lhs, wo[:, view], preferred_element_type=F32)
        for owner in range(head_count):
            proj[owner, :, view] = value[owner * head_tokens : (owner + 1) * head_tokens]
        for k in range(head_count - 1, 0, -1):
            proj_copy(index, width, k, head_peer(k), head).start()
    total = proj[head]
    for k in range(1, head_count):
        for index in range(chunks):
            proj_copy(index, width, k, head_peer(k), head_source(k)).wait_recv()
        total = total + proj_in[head_source(k)]
    out_ref[...] = total.astype(BF16)

    for k in range(1, head_count):
        norm_copy(k, head).wait_send()
        for index in range(chunks):
            proj_copy(index, width, k, head_peer(k), head).wait_send()
    for k in range(1, mem_count):
        for index, start, size in pieces:
            part_copy(index, start, size, k, mem_peer(k), mem).wait_send()
        heads_copy(k, mem).wait_send()
        stat_copy(k, mem).wait_send()
        accum_copy(k, mem_peer(k), mem).wait_send()
        att_copy(k, mem).wait_send()


def shards(
    hidden,
    norm_gain,
    q_weight,
    k_weight,
    v_weight,
    o_weight,
    k_cache,
    v_cache,
    page_table,
    attend_list,
    lengths,
):
    mem_count = lax.axis_size("mem")
    head_count = lax.axis_size("heads")
    features, q_cols = q_weight.shape
    kv_cols = k_weight.shape[1]
    _, local_kv, _, dim = k_cache.shape
    row_count = lengths.shape[0]
    tokens = hidden.shape[0] * head_count
    steps = tokens // row_count
    own_tokens = tokens // mem_count
    head_tokens = hidden.shape[0]
    local_heads = q_cols // dim
    per_kv = local_heads // local_kv
    out_cols = o_weight.shape[1]
    chunks = 4
    smem = pl.BlockSpec(memory_space=pltpu.SMEM)
    vmem = pl.BlockSpec(memory_space=pltpu.VMEM)
    hbm = pl.BlockSpec(memory_space=pl.ANY)
    dma = pltpu.SemaphoreType.DMA
    total_heads = local_heads + 2 * local_kv
    return pl.pallas_call(
        functools.partial(layer_kernel, mem_count, head_count, chunks),
        out_shape=jax.ShapeDtypeStruct((head_tokens, out_cols), BF16),
        in_specs=[smem] * 3 + [vmem] * 2 + [hbm] * 6,
        out_specs=vmem,
        scratch_shapes=[
            pltpu.VMEM(q_weight.shape, BF16),
            pltpu.VMEM(k_weight.shape, BF16),
            pltpu.VMEM(v_weight.shape, BF16),
            pltpu.VMEM(o_weight.shape, BF16),
            pltpu.VMEM(k_cache.shape, BF16),
            pltpu.VMEM(v_cache.shape, BF16),
            pltpu.VMEM((head_count, head_tokens, features), BF16),
            pltpu.VMEM((mem_count, own_tokens, q_cols + 2 * kv_cols), F32),
            pltpu.VMEM((mem_count, own_tokens, q_cols + 2 * kv_cols), F32),
            pltpu.VMEM((own_tokens, total_heads, dim), F32),
            pltpu.VMEM((mem_count, own_tokens, total_heads, dim), BF16),
            pltpu.VMEM((row_count, local_kv, steps * per_kv, dim), BF16),
            pltpu.VMEM((tokens, local_kv, per_kv, dim), F32),
            pltpu.VMEM((mem_count, own_tokens, local_kv, per_kv, dim), F32),
            pltpu.VMEM((mem_count, steps, per_kv, dim), F32),
            pltpu.VMEM((own_tokens, local_heads, dim), F32),
            pltpu.VMEM((mem_count, own_tokens, q_cols), BF16),
            pltpu.VMEM((head_count, head_tokens, out_cols), F32),
            pltpu.VMEM((head_count, head_tokens, out_cols), F32),
            dma((6, PIECES)),
            dma((head_count,)),
            dma((head_count,)),
            dma((chunks + 1, mem_count)),
            dma((chunks + 1, mem_count)),
            dma((mem_count,)),
            dma((mem_count,)),
            dma((mem_count,)),
            dma((mem_count,)),
            dma((mem_count,)),
            dma((mem_count,)),
            dma((mem_count,)),
            dma((mem_count,)),
            dma((chunks, head_count)),
            dma((chunks, head_count)),
        ],
        compiler_params=pltpu.CompilerParams(
            collective_id=0, has_side_effects=True, vmem_limit_bytes=60 * 1024 * 1024
        ),
    )(
        page_table,
        attend_list,
        lengths,
        hidden,
        norm_gain,
        q_weight,
        k_weight,
        v_weight,
        o_weight,
        k_cache,
        v_cache,
    )


def solution(mesh):
    in_specs = (
        P(("groups", "heads"), None),
        P("mem"),
        P("mem", "heads"),
        P("mem", "heads"),
        P("mem", "heads"),
        P("heads", "mem"),
        P(("groups", "mem"), "heads", None, None),
        P(("groups", "mem"), "heads", None, None),
        P("groups", None),
        P("groups", None),
        P("groups"),
    )
    out_specs = P(("groups", "heads"), "mem")
    return jax.shard_map(shards, mesh=mesh, in_specs=in_specs, out_specs=out_specs, check_vma=False)
```
